32 devices in a mesh: space: 4 (over y, core), mode: 8 (over z, x).
Axes of the slice: x: 2, y: 2, z: 4, core: 2. Of those that a mesh axis runs over, the one named last changes fastest.
Arguments:
- intensity: float32 [1024, 8, 64, 256], P('mode', None, 'space'), may hold values from 0.1 to 2
- dir_cos: float32 [3, 32], replicated, may hold values from -1 to 1, as said below
- velocity: float32 [32], replicated, may hold values from 0.2 to 1
- rate: float32 [32], replicated, may hold values from 0.05 to 2
- spectrum: float32 [32], replicated, may hold values from 0.2 to 2
- weight: float32 [32], replicated, may hold values from 0.25 to 1.75
- heat: float32 [64, 256], P('space'), may hold values from 0.5 to 4
- rough_cells: int32 [4096], P('space'), may hold values from 0 to 4095, as said below
- rough_count: int32 [4], P('space'), may hold values from 256 to 1024, as said below
- rough_map: int32 [4096, 16], P('space'), may hold values from 0 to 15
Outputs:
- intensity_new: float32 [1024, 8, 64, 256], P('mode', None, 'space')
- energy_new: float32 [8, 64, 256], P(None, 'space')
The draws below stay inside these ranges and needn't reach their ends.
Inputs may be any that keep to these rules, and one draw needn't show every extreme that they name: `dir_cos`: even directions have a positive third cosine, and direction 2k+1 equals direction 2k with the third cosine negated; every direction has a third cosine of magnitude 0.3 or more. `rough_cells`: the entries of one index of space are distinct. `rough_count`: some index of space has all 1024 slots live.
All inputs are finite; a program needn't handle non-finite values.
Results may differ from the reference program's by a relative error of at most 0.0015.
Values sent between devices are 32-bit elements; how exact they have to be, the bound alone decides.
A program may use at most 128 MiB of HBM per device.

```python
import math
import jax
import jax.numpy as jnp

DIRS = 32
MODES = 32
Z = 8
XR = 16
NY = 256
PAIRS = 1024
NX = 64
ROUGH = 1024
N_SPACE = 4


def draw_dir_cos(key, part):
    keys = jax.random.split(jax.random.fold_in(key, 11), 3)
    half = DIRS // 2
    ux = jax.random.normal(keys[0], (half,), jnp.float32)
    uy = jax.random.normal(keys[1], (half,), jnp.float32)
    uz = jax.random.uniform(keys[2], (half,), jnp.float32, 0.6, 1.6)
    length = jnp.sqrt(ux * ux + uy * uy + uz * uz)
    ux = ux / length
    uy = uy / length
    uz = jnp.maximum(uz / length, 0.3)
    cx = jnp.stack([ux, ux], axis=1).reshape(DIRS)
    cy = jnp.stack([uy, uy], axis=1).reshape(DIRS)
    cz = jnp.stack([uz, -uz], axis=1).reshape(DIRS)
    return jnp.stack([cx, cy, cz], axis=0).astype(jnp.float32)


def draw_rough_cells(key, part):
    keys = jax.random.split(jax.random.fold_in(key, 23), N_SPACE)
    lists = jax.vmap(lambda k: jax.random.permutation(k, XR * NY)[:ROUGH])(keys)
    return lists.reshape(-1).astype(jnp.int32)


def draw_rough_count(key, part):
    keys = jax.random.split(jax.random.fold_in(key, 37), 2)
    counts = jax.random.randint(keys[0], (N_SPACE,), ROUGH // 4, ROUGH + 1)
    fullest = jax.random.randint(keys[1], (), 0, N_SPACE)
    return counts.at[fullest].set(ROUGH).astype(jnp.int32)


def touch_ends(array, rng, smallest, top_value):
    spot = [jax.random.randint(jax.random.fold_in(rng, axis), (), 0, length) for axis, length in enumerate(array.shape)]
    main_axis = array.shape.index(max(array.shape))
    neighbour = spot[:main_axis] + [(spot[main_axis] + 1) % array.shape[main_axis]] + spot[main_axis + 1:]
    return array.at[tuple(spot)].set(smallest).at[tuple(neighbour)].set(top_value)


def block_levels(key, shape, cuts, least, largest):
    def one(position, parts):
        draws = jax.random.uniform(jax.random.fold_in(jax.random.fold_in(key, 6), position), (parts,), jnp.float32, least / len(cuts), largest / len(cuts))
        return jnp.repeat(jnp.exp(draws), shape[position] // parts).reshape((-1,) + (1,) * (len(shape) - position - 1))

    loudness = one(*cuts[0])
    for cut in cuts[1:]:
        loudness = loudness * one(*cut)
    return loudness


def setup_inputs(seed: int = 0) -> dict:
    seeds = jax.random.split(jax.random.key(seed), 11)
    return {
        "intensity": jnp.clip(jnp.exp(math.log(2.0) - 2.9957323 * jax.random.uniform(seeds[0], (PAIRS, Z, NX, NY), jnp.float32) ** block_levels(seeds[0], (PAIRS, Z, NX, NY), ((0, 8), (2, 4)), -0.2, 0.2)), 0.1, 2.0),
        "dir_cos": draw_dir_cos(jax.random.fold_in(seeds[10], 71), 0),
        "velocity": jnp.clip(jnp.exp(jax.random.uniform(seeds[2], (MODES,), jnp.float32, math.log(0.2), math.log(1.0))), 0.2, 1.0),
        "rate": jnp.clip(jnp.exp(jax.random.uniform(seeds[3], (MODES,), jnp.float32, math.log(0.05), math.log(2.0))), 0.05, 2.0),
        "spectrum": jnp.clip(jnp.exp(jax.random.uniform(seeds[4], (MODES,), jnp.float32, math.log(0.2), math.log(2.0))), 0.2, 2.0),
        "weight": jnp.clip(1.0 + 0.15 * jax.random.normal(seeds[5], (DIRS,), jnp.float32), 0.25, 1.75),
        "heat": jnp.clip(jnp.exp(math.log(4.0) - 2.0794415 * jax.random.uniform(seeds[6], (NX, NY), jnp.float32) ** block_levels(seeds[6], (NX, NY), ((0, 4),), -0.2, 0.2)), 0.5, 4.0),
        "rough_cells": draw_rough_cells(jax.random.fold_in(seeds[10], 71), 0),
        "rough_count": draw_rough_count(jax.random.fold_in(seeds[10], 71), 0),
        "rough_map": touch_ends(jax.random.randint(seeds[9], (N_SPACE * ROUGH, DIRS // 2), 0, DIRS // 2), jax.random.fold_in(seeds[9], 1), 0, (DIRS // 2) - 1).astype(jnp.int32),
    }


def drift_of(field, dir_cos, velocity):
    ox = dir_cos[0][:, None, None, None, None]
    oy = dir_cos[1][:, None, None, None, None]
    speed = velocity[None, :, None, None, None]
    padx = jnp.pad(field, ((0, 0), (0, 0), (0, 0), (1, 1), (0, 0)))
    pady = jnp.pad(field, ((0, 0), (0, 0), (0, 0), (0, 0), (1, 1)))
    along = jnp.maximum(ox, 0.0) * (field - padx[:, :, :, :-2]) + jnp.minimum(ox, 0.0) * (padx[:, :, :, 2:] - field)
    across = jnp.maximum(oy, 0.0) * (field - pady[..., :-2]) + jnp.minimum(oy, 0.0) * (pady[..., 2:] - field)
    return speed * (along + across)


def reference(intensity, dir_cos, velocity, rate, spectrum, weight, heat, rough_cells, rough_count, rough_map):
    field = intensity.reshape(DIRS, MODES, Z, NX, NY)
    energy = jnp.einsum('s,smzxy->zxy', weight, field) / PAIRS
    equil = energy / (1.0 + 0.3 * jnp.abs(energy))
    source = (rate * spectrum)[:, None, None, None] * equil[None]
    rhs = field + source[None] - drift_of(field, dir_cos, velocity)
    diag = 1.0 + rate
    couple = velocity[None, :] * jnp.abs(dir_cos[2])[:, None]
    up_rhs = rhs[0::2]
    down_rhs = rhs[1::2]
    cdown = couple[1::2][:, :, None, None]
    adown = diag[None, :, None, None] + cdown
    carry = spectrum[None, :, None, None] * heat[None, None]
    planes = [None] * Z
    for level in reversed(range(Z)):
        carry = (down_rhs[:, :, level] + cdown * carry) / adown
        planes[level] = carry
    down_new = jnp.stack(planes, axis=2)
    bottom = down_new[:, :, 0].reshape(DIRS // 2, MODES, NX * NY)
    offsets = jnp.arange(N_SPACE, dtype=jnp.int32) * (XR * NY)
    cells = (rough_cells.reshape(N_SPACE, ROUGH) + offsets[:, None]).reshape(-1).astype(jnp.int32)
    live = (jnp.arange(ROUGH, dtype=jnp.int32)[None, :] < rough_count[:, None]).reshape(-1)
    values = bottom[:, :, cells].transpose(2, 0, 1)
    picked = jnp.take_along_axis(values, rough_map[:, :, None], axis=1).transpose(1, 2, 0)
    current = bottom[:, :, cells]
    inflow = 0.9 * bottom.at[:, :, cells].set(jnp.where(live[None, None, :], picked, current))
    inflow = inflow.reshape(DIRS // 2, MODES, NX, NY)
    cup = couple[0::2][:, :, None, None]
    aup = diag[None, :, None, None] + cup
    carry = inflow
    planes = []
    for level in range(Z):
        carry = (up_rhs[:, :, level] + cup * carry) / aup
        planes.append(carry)
    up_new = jnp.stack(planes, axis=2)
    fresh = jnp.stack([up_new, down_new], axis=1).reshape(DIRS, MODES, Z, NX, NY)
    energy_new = jnp.einsum('s,smzxy->zxy', weight, fresh) / PAIRS
    return fresh.reshape(PAIRS, Z, NX, NY), energy_new
```

```python
import functools

import jax
import jax.numpy as jnp
from jax import lax
from jax.experimental import pallas as pl
from jax.experimental.pallas import tpu as pltpu
from jax.sharding import PartitionSpec as P

MESH = pl.DeviceIdType.MESH
F32 = jnp.float32
BF16 = jnp.bfloat16


def whole(space=pltpu.VMEM):
    return pl.BlockSpec(memory_space=space)


def squash(energy):
    return energy / (1.0 + 0.3 * jnp.abs(energy))


def send(src, dst, ssem, rsem, axis, target):
    return pltpu.make_async_remote_copy(
        src_ref=src,
        dst_ref=dst,
        send_sem=ssem,
        recv_sem=rsem,
        device_id={axis: target},
        device_id_type=MESH,
    )


def reduce_all(acc, slots, part, total, sems, n, finish):
    me = lax.axis_index("mode")
    rows = acc.shape[0] // n

    def chunk(i):
        return pl.ds(pl.multiple_of(i * rows, rows), rows)

    first = []
    for off in range(1, n):
        target = lax.rem(me + off, n)
        copy = send(
            acc.at[chunk(target)], slots.at[off], sems.at[0, off], sems.at[1, off], "mode", target
        )
        copy.start()
        first.append(copy)
    for copy in first:
        copy.wait_recv()
    value = acc[chunk(me), :]
    for off in range(1, n):
        value = value + slots[off]
    part[...] = finish(value)
    second = []
    for off in range(1, n):
        target = lax.rem(me + off, n)
        copy = send(part, total.at[chunk(me)], sems.at[2, off], sems.at[3, off], "mode", target)
        copy.start()
        second.append(copy)
    total[chunk(me), :] = part[...]
    for copy in first:
        copy.wait_send()
    for off in range(1, n):
        source = lax.rem(me + n - off, n)
        send(
            part, total.at[chunk(source)], sems.at[2, off], sems.at[3, off], "mode", source
        ).wait_recv()
    for copy in second:
        copy.wait_send()


def greet_modes(barrier, n):
    me = lax.axis_index("mode")
    for off in range(1, n):
        pl.semaphore_signal(
            barrier, inc=1, device_id={"mode": lax.rem(me + off, n)}, device_id_type=MESH
        )


def open_kernel(
    n, ns, modes, planes, pairs_total,
    weight, x_ref, equil, lo_out, hi_out,
    acc, slots, part, total, row_first, row_last, hsem, sems,
):
    step = pl.program_id(0)
    steps = pl.num_programs(0)
    block = x_ref.shape[0]
    rows = x_ref.shape[1]
    per_plane = rows // planes
    me = lax.axis_index("mode")
    sp = lax.axis_index("space")
    dirs_local = lo_out.shape[0] // modes

    @pl.when(step == 0)
    def _():
        barrier = pltpu.get_barrier_semaphore()
        greet_modes(barrier, n)

        @pl.when(sp > 0)
        def _():
            pl.semaphore_signal(barrier, inc=1, device_id={"space": sp - 1}, device_id_type=MESH)

        @pl.when(sp < ns - 1)
        def _():
            pl.semaphore_signal(barrier, inc=1, device_id={"space": sp + 1}, device_id_type=MESH)

        low = jnp.where(sp > 0, 1, 0)
        high = jnp.where(sp < ns - 1, 1, 0)
        pl.semaphore_wait(barrier, n - 1 + low + high)
        acc[...] = jnp.zeros_like(acc)

    part_of = pl.ds(step * block, block)
    has_low = jnp.where(sp > 0, 1.0, 0.0)
    has_high = jnp.where(sp < ns - 1, 1.0, 0.0)

    def edges(p, carry):
        for z in range(planes):
            first, last = z * per_plane, (z + 1) * per_plane - 1
            row_first[step * block + p, pl.ds(z, 1), :] = x_ref[p, pl.ds(first, 1), :] * has_low
            row_last[step * block + p, pl.ds(z, 1), :] = x_ref[p, pl.ds(last, 1), :] * has_high
        return carry

    lax.fori_loop(0, block, edges, 0)

    def down_copy(g):
        where = pl.ds(g * block, block)
        return send(
            row_first.at[where], hi_out.at[where], hsem.at[0, g], hsem.at[1, g], "space",
            lax.rem(sp + ns - 1, ns),
        )

    def up_copy(g):
        where = pl.ds(g * block, block)
        return send(
            row_last.at[where], lo_out.at[where], hsem.at[2, g], hsem.at[3, g], "space",
            lax.rem(sp + 1, ns),
        )

    def low_zero(g):
        where = pl.ds(g * block, block)
        return pltpu.make_async_copy(row_first.at[where], lo_out.at[where], hsem.at[3, g])

    def high_zero(g):
        where = pl.ds(g * block, block)
        return pltpu.make_async_copy(row_last.at[where], hi_out.at[where], hsem.at[1, g])

    @pl.when(sp > 0)
    def _():
        down_copy(step).start()

    @pl.when(sp == 0)
    def _():
        low_zero(step).start()

    @pl.when(sp < ns - 1)
    def _():
        up_copy(step).start()

    @pl.when(sp == ns - 1)
    def _():
        high_zero(step).start()

    w = weight[me * dirs_local + step * block // modes]

    def add_rows(r, carry):
        here = pl.ds(pl.multiple_of(r * 8, 8), 8)
        value = x_ref[0, here, :]
        for p in range(1, block):
            value = value + x_ref[p, here, :]
        acc[here, :] += w * value
        return carry

    lax.fori_loop(0, rows // 8, add_rows, 0)

    @pl.when(step == steps - 1)
    def _():
        reduce_all(
            acc, slots, part, total, sems, n, lambda value: squash(value * (1.0 / pairs_total))
        )
        equil[...] = total[...]

        def finish(g, carry):
            @pl.when(sp > 0)
            def _():
                down_copy(g).wait_send()
                up_copy(g).wait_recv()

            @pl.when(sp == 0)
            def _():
                low_zero(g).wait()

            @pl.when(sp < ns - 1)
            def _():
                up_copy(g).wait_send()
                down_copy(g).wait_recv()

            @pl.when(sp == ns - 1)
            def _():
                high_zero(g).wait()

            return carry

        lax.fori_loop(0, lo_out.shape[0] // block, finish, 0)


def open_step(x, weight, n, ns, modes, planes, pairs_total):
    pairs, rows, width = x.shape
    block = 16
    halo = jax.ShapeDtypeStruct((pairs, planes, width), F32)
    return pl.pallas_call(
        functools.partial(open_kernel, n, ns, modes, planes, pairs_total),
        grid=(pairs // block,),
        out_shape=(jax.ShapeDtypeStruct((rows, width), F32), halo, halo),
        in_specs=[whole(pltpu.SMEM), pl.BlockSpec((block, rows, width), lambda i: (i, 0, 0))],
        out_specs=(pl.BlockSpec((rows, width), lambda i: (0, 0)), whole(pl.ANY), whole(pl.ANY)),
        scratch_shapes=[
            pltpu.VMEM((rows, width), F32),
            pltpu.VMEM((n, rows // n, width), F32),
            pltpu.VMEM((rows // n, width), F32),
            pltpu.VMEM((rows, width), F32),
            pltpu.VMEM((pairs, planes, width), F32),
            pltpu.VMEM((pairs, planes, width), F32),
            pltpu.SemaphoreType.DMA((4, pairs // block)),
            pltpu.SemaphoreType.DMA((4, n)),
        ],
        compiler_params=pltpu.CompilerParams(collective_id=0, has_side_effects=True),
        name="open_step",
    )(weight, x)


def close_kernel(n, pairs_total, x_ref, out, slots, part, total, sems):
    barrier = pltpu.get_barrier_semaphore()
    greet_modes(barrier, n)
    pl.semaphore_wait(barrier, n - 1)
    reduce_all(x_ref, slots, part, total, sems, n, lambda value: value * (1.0 / pairs_total))
    out[...] = total[...]


def close_step(x, n, pairs_total):
    rows, width = x.shape
    return pl.pallas_call(
        functools.partial(close_kernel, n, pairs_total),
        out_shape=jax.ShapeDtypeStruct((rows, width), F32),
        in_specs=[whole()],
        out_specs=whole(),
        scratch_shapes=[
            pltpu.VMEM((n, rows // n, width), F32),
            pltpu.VMEM((rows // n, width), F32),
            pltpu.VMEM((rows, width), F32),
            pltpu.SemaphoreType.DMA((4, n)),
        ],
        compiler_params=pltpu.CompilerParams(collective_id=1, has_side_effects=True),
        name="close_step",
    )(x)


def split(value):
    high = value.astype(BF16)
    return high, (value - high.astype(F32)).astype(BF16)


def rough_kernel(n, count, bottom, cells, targets, inflow, held, picked, marks, ssem, rsem):
    me = lax.axis_index("mode")
    pairs, rows, width = bottom.shape
    slots = cells.shape[1]
    half = targets.shape[0]
    modes = pairs // half

    def place_of(index):
        return jnp.where(lax.rem(index, 2) == 0, index // 2, n - 1 - index // 2)

    def index_of(place):
        place = lax.rem(place + n, n)
        return jnp.where(place < n // 2, 2 * place, 2 * (n - 1 - place) + 1)

    place = place_of(me)
    ends = (index_of(place + 1), index_of(place - 1))
    barrier = pltpu.get_barrier_semaphore()
    for target in ends:
        pl.semaphore_signal(barrier, inc=1, device_id={"mode": target}, device_id_type=MESH)

    marks[...] = jnp.where(
        lax.broadcasted_iota(jnp.int32, (width, slots), 0) == lax.rem(cells[...], width), 1.0, 0.0
    ).astype(BF16)
    row_of = cells[...] // width
    on_row = jnp.where(lax.broadcasted_iota(jnp.int32, (rows, slots), 0) == row_of, 1.0, 0.0)

    group = min(16, pairs)

    def gather(g, carry):
        here = pl.ds(pl.multiple_of(g * group, group), group)
        high, low = split(bottom[here].reshape(group * rows, width))
        column = marks[...]
        got = jnp.dot(high, column, preferred_element_type=F32) + jnp.dot(
            low, column, preferred_element_type=F32
        )
        held[place, here, :] = jnp.sum(got.reshape(group, rows, slots) * on_row[None], axis=1)
        return carry

    lax.fori_loop(0, pairs // group, gather, 0)
    pl.semaphore_wait(barrier, 2)

    piece = pairs // 4

    def copy_of(way, part, step):
        slot = lax.rem(place + n + (-step if way == 0 else step), n)
        at = held.at[slot, pl.ds((2 * way + part) * piece, piece)]
        return send(at, at, ssem.at[way, part, step], rsem.at[way, part, step], "mode", ends[way])

    for step in range(n - 1):
        for part in range(2):
            for way in range(2):
                if step > 0:
                    arrived(copy_of, n, place, held, ssem, rsem, way, part, step - 1, piece, ends)
                copy_of(way, part, step).start()
    for part in range(2):
        for way in range(2):
            arrived(copy_of, n, place, held, ssem, rsem, way, part, n - 2, piece, ends)
    for step in range(n - 1):
        for part in range(2):
            for way in range(2):
                copy_of(way, part, step).wait_send()

    for h in range(half):
        want = targets[pl.ds(h, 1), :]
        for m in range(0, modes, 8):
            value = jnp.zeros((8, slots), F32)
            for p in range(n):
                owner = 2 * p if p < n // 2 else 2 * (n - 1 - p) + 1
                for j in range(half):
                    value = jnp.where(
                        want == owner * half + j, held[p, pl.ds(j * modes + m, 8), :], value
                    )
            picked[pl.ds(h * modes + m, 8), :] = value

    live = jnp.where(lax.broadcasted_iota(jnp.int32, (rows, slots), 1) < count[0], on_row, 0.0)
    contract = (((1,), (1,)), ((), ()))
    is_rough = lax.dot_general(live.astype(BF16), marks[...], contract, preferred_element_type=F32)
    is_rough = (is_rough > 0.5)[None]

    def scatter(g, carry):
        here = pl.ds(pl.multiple_of(g * group, group), group)
        spread = (picked[here, :][:, None, :] * live[None]).reshape(group * rows, slots)
        high, low = split(spread)
        column = marks[...]
        put = lax.dot_general(
            high, column, contract, preferred_element_type=F32
        ) + lax.dot_general(low, column, contract, preferred_element_type=F32)
        inflow[here] = 0.9 * jnp.where(is_rough, put.reshape(group, rows, width), bottom[here])
        return carry

    lax.fori_loop(0, pairs // group, scatter, 0)


def arrived(copy_of, n, place, held, ssem, rsem, way, part, step, piece, ends):
    slot = lax.rem(place + n + (-step - 1 if way == 0 else step + 1), n)
    at = held.at[slot, pl.ds((2 * way + part) * piece, piece)]
    send(
        at, at, ssem.at[way, part, step], rsem.at[way, part, step], "mode", ends[way]
    ).wait_recv()


def rough_step(bottom, cells, count, targets, n):
    pairs, rows, width = bottom.shape
    slots = cells.shape[1]
    return pl.pallas_call(
        functools.partial(rough_kernel, n),
        out_shape=jax.ShapeDtypeStruct(bottom.shape, F32),
        in_specs=[whole(pltpu.SMEM), whole(), whole(), whole()],
        out_specs=whole(),
        scratch_shapes=[
            pltpu.VMEM((n, pairs, slots), F32),
            pltpu.VMEM((pairs, slots), F32),
            pltpu.VMEM((width, slots), BF16),
            pltpu.SemaphoreType.DMA((2, 2, n - 1)),
            pltpu.SemaphoreType.DMA((2, 2, n - 1)),
        ],
        compiler_params=pltpu.CompilerParams(collective_id=2, has_side_effects=True),
        name="rough_step",
    )(count, bottom, cells, targets)


def sweep_kernel(down, planes, *refs):
    if down:
        (dir_cos, velocity, rate, spectrum, weight, x_ref, lo, hi, equil, start, out, bottom,
         energy) = refs
    else:
        (dir_cos, velocity, rate, spectrum, weight, x_ref, lo, hi, equil, start, before, _,
         out, energy) = refs
    h, b = pl.program_id(0), pl.program_id(1)
    count, total_rows, width = x_ref.shape
    rows = total_rows // planes

    @pl.when((h == 0) & (b == 0))
    def _():
        energy[...] = jnp.zeros_like(energy) if down else before[...]

    s = (lax.axis_index("mode") * pl.num_programs(0) + h) * 2 + (1 if down else 0)
    cx, cy, cz = dir_cos[0, s], dir_cos[1, s], dir_cos[2, s]
    w = weight[s]
    row = lax.broadcasted_iota(jnp.int32, (rows, width), 0)
    lane = lax.broadcasted_iota(jnp.int32, (rows, width), 1)

    def run(low_x, low_y):
        def one(i, carry):
            m = b * count + i
            v = velocity[m]
            c = v * jnp.abs(cz)
            inv = 1.0 / jnp.full((rows, width), 1.0 + rate[m] + c, F32)
            vx, vy = v * jnp.abs(cx), v * jnp.abs(cy)
            k_own, k_x, k_y = inv * (1.0 - vx - vy), inv * vx, inv * vy
            k_src, k_prev = inv * (rate[m] * spectrum[m]), inv * c
            k_y = jnp.where(lane == (0 if low_y else width - 1), 0.0, k_y)
            if down:
                value = start[...] * spectrum[m]
            else:
                value = start[i]
            for z in reversed(range(planes)) if down else range(planes):
                here = pl.ds(z * rows, rows)
                own = x_ref[i, here, :]
                edge = (lo if low_x else hi)[i, pl.ds(z, 1), :]
                if low_x:
                    side = jnp.where(row == 0, edge, pltpu.roll(own, 1, 0))
                else:
                    side = jnp.where(row == rows - 1, edge, pltpu.roll(own, rows - 1, 0))
                along = pltpu.roll(own, 1 if low_y else width - 1, 1)
                value = (
                    k_own * own + k_x * side + k_y * along + k_src * equil[here, :]
                    + k_prev * value
                )
                out[i, here, :] = value
                energy[here, :] += w * value
            if down:
                bottom[i] = value
            return carry

        lax.fori_loop(0, count, one, 0)

    for low_x in (True, False):
        for low_y in (True, False):
            @pl.when(((cx >= 0) == low_x) & ((cy >= 0) == low_y))
            def _():
                run(low_x, low_y)


def sweep_step(down, planes, scalars, x, lo, hi, equil, start, before=None, aliased=None):
    half, _, modes, total_rows, width = x.shape
    rows = total_rows // planes
    block = min(8, modes)
    side = 1 if down else 0
    big = pl.BlockSpec((None, None, block, total_rows, width), lambda h, b: (h, side, b, 0, 0))
    edge = pl.BlockSpec((None, None, block, planes, width), lambda h, b: (h, side, b, 0, 0))
    flat = pl.BlockSpec((total_rows, width), lambda h, b: (0, 0))
    floor = pl.BlockSpec((None, block, rows, width), lambda h, b: (h, b, 0, 0))
    heat = pl.BlockSpec((rows, width), lambda h, b: (0, 0))
    in_specs = [whole(pltpu.SMEM)] * len(scalars) + [big, edge, edge, flat]
    flat_shape = jax.ShapeDtypeStruct((total_rows, width), F32)
    floor_shape = jax.ShapeDtypeStruct((half, modes, rows, width), F32)
    args = [*scalars, x, lo, hi, equil, start]
    if down:
        in_specs += [heat]
        out_shape = (jax.ShapeDtypeStruct(x.shape, F32), floor_shape, flat_shape)
        out_specs = (big, floor, flat)
        aliases = {}
    else:
        in_specs += [floor, flat, whole(pl.ANY)]
        args += [before, aliased]
        out_shape = (jax.ShapeDtypeStruct(x.shape, F32), flat_shape)
        out_specs = (big, flat)
        aliases = {len(args) - 1: 0}
    return pl.pallas_call(
        functools.partial(sweep_kernel, down, planes),
        grid=(half, modes // block),
        out_shape=out_shape,
        in_specs=in_specs,
        out_specs=out_specs,
        input_output_aliases=aliases,
        name="down_sweep" if down else "up_sweep",
    )(*args)


def per_device(
    n, ns, intensity, dir_cos, velocity, rate, spectrum, weight, heat, rough_cells, rough_count,
    rough_map,
):
    pairs, planes, rows, width = intensity.shape
    modes = velocity.shape[0]
    half = pairs // modes // 2
    pairs_total = pairs * n
    position = lax.axis_index("mode")
    flat = intensity.reshape(pairs, planes * rows, width)
    equil, lo, hi = open_step(flat, weight, n, ns, modes, planes, pairs_total)
    x = intensity.reshape(half, 2, modes, planes * rows, width)
    lo = lo.reshape(half, 2, modes, planes, width)
    hi = hi.reshape(half, 2, modes, planes, width)
    scalars = (dir_cos, velocity, rate, spectrum, weight)
    fresh, bottom, energy = sweep_step(True, planes, scalars, x, lo, hi, equil, heat)
    targets = lax.dynamic_slice_in_dim(rough_map, position * half, half, 1).T
    inflow = rough_step(
        bottom.reshape(half * modes, rows, width), rough_cells[None], rough_count, targets, n
    )
    inflow = inflow.reshape(half, modes, rows, width)
    fresh, energy = sweep_step(
        False, planes, scalars, x, lo, hi, equil, inflow, energy, fresh
    )
    energy = close_step(energy, n, pairs_total)
    return fresh.reshape(intensity.shape), energy.reshape(planes, rows, width)


def solution(mesh):
    n, ns = mesh.shape["mode"], mesh.shape["space"]
    in_specs = (
        P("mode", None, "space", None),
        P(),
        P(),
        P(),
        P(),
        P(),
        P("space", None),
        P("space"),
        P("space"),
        P("space", None),
    )
    out_specs = (P("mode", None, "space", None), P(None, "space", None))
    return jax.shard_map(
        functools.partial(per_device, n, ns),
        mesh=mesh,
        in_specs=in_specs,
        out_specs=out_specs,
        check_vma=False,
    )
```

```python
import functools

import jax
import jax.numpy as jnp
from jax import lax
from jax.experimental import pallas as pl
from jax.experimental.pallas import tpu as pltpu
from jax.sharding import PartitionSpec as P

MESH = pl.DeviceIdType.MESH
F32 = jnp.float32
BF16 = jnp.bfloat16


def whole(space=pltpu.VMEM):
    return pl.BlockSpec(memory_space=space)


def squash(energy):
    return energy / (1.0 + 0.3 * jnp.abs(energy))


def send(src, dst, ssem, rsem, axis, target):
    return pltpu.make_async_remote_copy(
        src_ref=src,
        dst_ref=dst,
        send_sem=ssem,
        recv_sem=rsem,
        device_id={axis: target},
        device_id_type=MESH,
    )


def reduce_all(acc, slots, part, total, sems, n, finish):
    me = lax.axis_index("mode")
    rows = acc.shape[0] // n

    def chunk(i):
        return pl.ds(pl.multiple_of(i * rows, rows), rows)

    first = []
    for off in range(1, n):
        target = lax.rem(me + off, n)
        copy = send(
            acc.at[chunk(target)], slots.at[off], sems.at[0, off], sems.at[1, off], "mode", target
        )
        copy.start()
        first.append(copy)
    for copy in first:
        copy.wait_recv()
    value = acc[chunk(me), :]
    for off in range(1, n):
        value = value + slots[off]
    part[...] = finish(value)
    second = []
    for off in range(1, n):
        target = lax.rem(me + off, n)
        copy = send(part, total.at[chunk(me)], sems.at[2, off], sems.at[3, off], "mode", target)
        copy.start()
        second.append(copy)
    total[chunk(me), :] = part[...]
    for copy in first:
        copy.wait_send()
    for off in range(1, n):
        source = lax.rem(me + n - off, n)
        send(
            part, total.at[chunk(source)], sems.at[2, off], sems.at[3, off], "mode", source
        ).wait_recv()
    for copy in second:
        copy.wait_send()


def greet_modes(barrier, n):
    me = lax.axis_index("mode")
    for off in range(1, n):
        pl.semaphore_signal(
            barrier, inc=1, device_id={"mode": lax.rem(me + off, n)}, device_id_type=MESH
        )


def open_kernel(
    n, ns, modes, planes, pairs_total,
    weight, x_ref, equil, lo_out, hi_out,
    acc, slots, part, total, row_first, row_last, hsem, sems,
):
    step = pl.program_id(0)
    steps = pl.num_programs(0)
    block = x_ref.shape[0]
    rows = x_ref.shape[1]
    per_plane = rows // planes
    me = lax.axis_index("mode")
    sp = lax.axis_index("space")
    dirs_local = lo_out.shape[0] // modes

    @pl.when(step == 0)
    def _():
        barrier = pltpu.get_barrier_semaphore()
        greet_modes(barrier, n)

        @pl.when(sp > 0)
        def _():
            pl.semaphore_signal(barrier, inc=1, device_id={"space": sp - 1}, device_id_type=MESH)

        @pl.when(sp < ns - 1)
        def _():
            pl.semaphore_signal(barrier, inc=1, device_id={"space": sp + 1}, device_id_type=MESH)

        low = jnp.where(sp > 0, 1, 0)
        high = jnp.where(sp < ns - 1, 1, 0)
        pl.semaphore_wait(barrier, n - 1 + low + high)
        acc[...] = jnp.zeros_like(acc)

    part_of = pl.ds(step * block, block)
    has_low = jnp.where(sp > 0, 1.0, 0.0)
    has_high = jnp.where(sp < ns - 1, 1.0, 0.0)

    def edges(p, carry):
        for z in range(planes):
            first, last = z * per_plane, (z + 1) * per_plane - 1
            row_first[step * block + p, pl.ds(z, 1), :] = x_ref[p, pl.ds(first, 1), :] * has_low
            row_last[step * block + p, pl.ds(z, 1), :] = x_ref[p, pl.ds(last, 1), :] * has_high
        return carry

    lax.fori_loop(0, block, edges, 0)

    def down_copy(g):
        where = pl.ds(g * block, block)
        return send(
            row_first.at[where], hi_out.at[where], hsem.at[0, g], hsem.at[1, g], "space",
            lax.rem(sp + ns - 1, ns),
        )

    def up_copy(g):
        where = pl.ds(g * block, block)
        return send(
            row_last.at[where], lo_out.at[where], hsem.at[2, g], hsem.at[3, g], "space",
            lax.rem(sp + 1, ns),
        )

    def low_zero(g):
        where = pl.ds(g * block, block)
        return pltpu.make_async_copy(row_first.at[where], lo_out.at[where], hsem.at[3, g])

    def high_zero(g):
        where = pl.ds(g * block, block)
        return pltpu.make_async_copy(row_last.at[where], hi_out.at[where], hsem.at[1, g])

    @pl.when(sp > 0)
    def _():
        down_copy(step).start()

    @pl.when(sp == 0)
    def _():
        low_zero(step).start()

    @pl.when(sp < ns - 1)
    def _():
        up_copy(step).start()

    @pl.when(sp == ns - 1)
    def _():
        high_zero(step).start()

    w = weight[me * dirs_local + step * block // modes]

    def add_rows(r, carry):
        here = pl.ds(pl.multiple_of(r * 8, 8), 8)
        value = x_ref[0, here, :]
        for p in range(1, block):
            value = value + x_ref[p, here, :]
        acc[here, :] += w * value
        return carry

    lax.fori_loop(0, rows // 8, add_rows, 0)

    @pl.when(step == steps - 1)
    def _():
        reduce_all(
            acc, slots, part, total, sems, n, lambda value: squash(value * (1.0 / pairs_total))
        )
        equil[...] = total[...]

        def finish(g, carry):
            @pl.when(sp > 0)
            def _():
                down_copy(g).wait_send()
                up_copy(g).wait_recv()

            @pl.when(sp == 0)
            def _():
                low_zero(g).wait()

            @pl.when(sp < ns - 1)
            def _():
                up_copy(g).wait_send()
                down_copy(g).wait_recv()

            @pl.when(sp == ns - 1)
            def _():
                high_zero(g).wait()

            return carry

        lax.fori_loop(0, lo_out.shape[0] // block, finish, 0)


def open_step(x, weight, n, ns, modes, planes, pairs_total):
    pairs, rows, width = x.shape
    block = 16
    halo = jax.ShapeDtypeStruct((pairs, planes, width), F32)
    return pl.pallas_call(
        functools.partial(open_kernel, n, ns, modes, planes, pairs_total),
        grid=(pairs // block,),
        out_shape=(jax.ShapeDtypeStruct((rows, width), F32), halo, halo),
        in_specs=[whole(pltpu.SMEM), pl.BlockSpec((block, rows, width), lambda i: (i, 0, 0))],
        out_specs=(pl.BlockSpec((rows, width), lambda i: (0, 0)), whole(pl.ANY), whole(pl.ANY)),
        scratch_shapes=[
            pltpu.VMEM((rows, width), F32),
            pltpu.VMEM((n, rows // n, width), F32),
            pltpu.VMEM((rows // n, width), F32),
            pltpu.VMEM((rows, width), F32),
            pltpu.VMEM((pairs, planes, width), F32),
            pltpu.VMEM((pairs, planes, width), F32),
            pltpu.SemaphoreType.DMA((4, pairs // block)),
            pltpu.SemaphoreType.DMA((4, n)),
        ],
        compiler_params=pltpu.CompilerParams(collective_id=0, has_side_effects=True),
        name="open_step",
    )(weight, x)


def close_kernel(n, pairs_total, x_ref, out, slots, part, total, sems):
    barrier = pltpu.get_barrier_semaphore()
    greet_modes(barrier, n)
    pl.semaphore_wait(barrier, n - 1)
    reduce_all(x_ref, slots, part, total, sems, n, lambda value: value * (1.0 / pairs_total))
    out[...] = total[...]


def close_step(x, n, pairs_total):
    rows, width = x.shape
    return pl.pallas_call(
        functools.partial(close_kernel, n, pairs_total),
        out_shape=jax.ShapeDtypeStruct((rows, width), F32),
        in_specs=[whole()],
        out_specs=whole(),
        scratch_shapes=[
            pltpu.VMEM((n, rows // n, width), F32),
            pltpu.VMEM((rows // n, width), F32),
            pltpu.VMEM((rows, width), F32),
            pltpu.SemaphoreType.DMA((4, n)),
        ],
        compiler_params=pltpu.CompilerParams(collective_id=1, has_side_effects=True),
        name="close_step",
    )(x)


def split(value):
    high = value.astype(BF16)
    return high, (value - high.astype(F32)).astype(BF16)


def rough_kernel(n, count, bottom, cells, targets, inflow, held, picked, marks, ssem, rsem):
    me = lax.axis_index("mode")
    pairs, rows, width = bottom.shape
    slots = cells.shape[1]
    half = targets.shape[0]
    modes = pairs // half

    def place_of(index):
        return jnp.where(lax.rem(index, 2) == 0, index // 2, n - 1 - index // 2)

    def index_of(place):
        place = lax.rem(place + n, n)
        return jnp.where(place < n // 2, 2 * place, 2 * (n - 1 - place) + 1)

    place = place_of(me)
    ends = (index_of(place + 1), index_of(place - 1))
    barrier = pltpu.get_barrier_semaphore()
    for target in ends:
        pl.semaphore_signal(barrier, inc=1, device_id={"mode": target}, device_id_type=MESH)

    marks[...] = jnp.where(
        lax.broadcasted_iota(jnp.int32, (width, slots), 0) == lax.rem(cells[...], width), 1.0, 0.0
    ).astype(BF16)
    row_of = cells[...] // width
    on_row = jnp.where(lax.broadcasted_iota(jnp.int32, (rows, slots), 0) == row_of, 1.0, 0.0)

    piece = pairs // 4

    def rows_of(way, part):
        return (2 * way + part) * piece

    def gather(first):
        here = pl.ds(first, piece)
        high, low = split(bottom[here].reshape(piece * rows, width))
        column = marks[...]
        got = jnp.dot(high, column, preferred_element_type=F32) + jnp.dot(
            low, column, preferred_element_type=F32
        )
        held[place, here, :] = jnp.sum(got.reshape(piece, rows, slots) * on_row[None], axis=1)

    def slot_of(way, step):
        return lax.rem(place + n + (-step if way == 0 else step), n)

    def copy_of(way, part, step):
        at = held.at[slot_of(way, step), pl.ds(rows_of(way, part), piece)]
        return send(at, at, ssem.at[way, part, step], rsem.at[way, part, step], "mode", ends[way])

    def arrival(way, part, step):
        at = held.at[slot_of(way, step + 1), pl.ds(rows_of(way, part), piece)]
        return send(at, at, ssem.at[way, part, step], rsem.at[way, part, step], "mode", ends[way])

    def choose(way, step):
        slot = slot_of(way, step)
        owner = index_of(slot)
        for h in range(half):
            want = targets[pl.ds(h, 1), :]
            for first in range(rows_of(way, 0), rows_of(way, 0) + 2 * piece, 8):
                j, m = first // modes, first % modes
                here = pl.ds(h * modes + m, 8)
                picked[here, :] = jnp.where(
                    want == owner * half + j, held[slot, pl.ds(first, 8), :], picked[here, :]
                )

    for part in range(2):
        for way in range(2):
            gather(rows_of(way, part))
            if part == 0 and way == 0:
                pl.semaphore_wait(barrier, 2)
            copy_of(way, part, 0).start()
    picked[...] = jnp.zeros_like(picked)
    for way in range(2):
        choose(way, 0)
    for step in range(1, n):
        for part in range(2):
            for way in range(2):
                arrival(way, part, step - 1).wait_recv()
                if step < n - 1:
                    copy_of(way, part, step).start()
        for way in range(2):
            choose(way, step)
    for step in range(n - 1):
        for part in range(2):
            for way in range(2):
                copy_of(way, part, step).wait_send()

    group = piece
    live = jnp.where(lax.broadcasted_iota(jnp.int32, (rows, slots), 1) < count[0], on_row, 0.0)
    contract = (((1,), (1,)), ((), ()))
    is_rough = lax.dot_general(live.astype(BF16), marks[...], contract, preferred_element_type=F32)
    is_rough = (is_rough > 0.5)[None]

    def scatter(g, carry):
        here = pl.ds(pl.multiple_of(g * group, group), group)
        spread = (picked[here, :][:, None, :] * live[None]).reshape(group * rows, slots)
        high, low = split(spread)
        column = marks[...]
        put = lax.dot_general(
            high, column, contract, preferred_element_type=F32
        ) + lax.dot_general(low, column, contract, preferred_element_type=F32)
        inflow[here] = 0.9 * jnp.where(is_rough, put.reshape(group, rows, width), bottom[here])
        return carry

    lax.fori_loop(0, pairs // group, scatter, 0)


def rough_step(bottom, cells, count, targets, n):
    pairs, rows, width = bottom.shape
    slots = cells.shape[1]
    return pl.pallas_call(
        functools.partial(rough_kernel, n),
        out_shape=jax.ShapeDtypeStruct(bottom.shape, F32),
        in_specs=[whole(pltpu.SMEM), whole(), whole(), whole()],
        out_specs=whole(),
        scratch_shapes=[
            pltpu.VMEM((n, pairs, slots), F32),
            pltpu.VMEM((pairs, slots), F32),
            pltpu.VMEM((width, slots), BF16),
            pltpu.SemaphoreType.DMA((2, 2, n - 1)),
            pltpu.SemaphoreType.DMA((2, 2, n - 1)),
        ],
        compiler_params=pltpu.CompilerParams(collective_id=2, has_side_effects=True),
        name="rough_step",
    )(count, bottom, cells, targets)


def sweep_kernel(down, planes, *refs):
    if down:
        (dir_cos, velocity, rate, spectrum, weight, x_ref, lo, hi, equil, start, out, bottom,
         energy) = refs
    else:
        (dir_cos, velocity, rate, spectrum, weight, x_ref, lo, hi, equil, start, before, _,
         out, energy) = refs
    h, b = pl.program_id(0), pl.program_id(1)
    count, total_rows, width = x_ref.shape
    rows = total_rows // planes

    @pl.when((h == 0) & (b == 0))
    def _():
        energy[...] = jnp.zeros_like(energy) if down else before[...]

    s = (lax.axis_index("mode") * pl.num_programs(0) + h) * 2 + (1 if down else 0)
    cx, cy, cz = dir_cos[0, s], dir_cos[1, s], dir_cos[2, s]
    w = weight[s]
    row = lax.broadcasted_iota(jnp.int32, (rows, width), 0)
    lane = lax.broadcasted_iota(jnp.int32, (rows, width), 1)

    wide = min(4, count)

    def run(low_x, low_y):
        def some(g, carry):
            picks = [g * wide + t for t in range(wide)]
            own_k, x_k, y_k, src_k, prev_k, values = [], [], [], [], [], []
            for i in picks:
                m = b * count + i
                v = velocity[m]
                c = v * jnp.abs(cz)
                inv = 1.0 / jnp.full((rows, width), 1.0 + rate[m] + c, F32)
                vx, vy = v * jnp.abs(cx), v * jnp.abs(cy)
                own_k.append(inv * (1.0 - vx - vy))
                x_k.append(inv * vx)
                y_k.append(inv * vy)
                src_k.append(inv * (rate[m] * spectrum[m]))
                prev_k.append(inv * c)
                values.append(start[...] * spectrum[m] if down else start[i])
            for z in reversed(range(planes)) if down else range(planes):
                here = pl.ds(z * rows, rows)
                level = equil[here, :]
                total = None
                for t, i in enumerate(picks):
                    own = x_ref[i, here, :]
                    edge = (lo if low_x else hi)[i, pl.ds(z, 1), :]
                    if low_x:
                        side = jnp.where(row == 0, edge, pltpu.roll(own, 1, 0))
                    else:
                        side = jnp.where(row == rows - 1, edge, pltpu.roll(own, rows - 1, 0))
                    along = pltpu.roll(own, 1 if low_y else width - 1, 1)
                    along = jnp.where(lane == (0 if low_y else width - 1), 0.0, along)
                    value = (
                        own_k[t] * own + x_k[t] * side + y_k[t] * along + src_k[t] * level
                        + prev_k[t] * values[t]
                    )
                    values[t] = value
                    out[i, here, :] = value
                    total = value if total is None else total + value
                energy[here, :] += w * total
            if down:
                for t, i in enumerate(picks):
                    bottom[i] = values[t]
            return carry

        lax.fori_loop(0, count // wide, some, 0)

    for low_x in (True, False):
        for low_y in (True, False):
            @pl.when(((cx >= 0) == low_x) & ((cy >= 0) == low_y))
            def _():
                run(low_x, low_y)


def sweep_step(down, planes, scalars, x, lo, hi, equil, start, before=None, aliased=None):
    half, _, modes, total_rows, width = x.shape
    rows = total_rows // planes
    block = min(8, modes)
    side = 1 if down else 0
    big = pl.BlockSpec((None, None, block, total_rows, width), lambda h, b: (h, side, b, 0, 0))
    edge = pl.BlockSpec((None, None, block, planes, width), lambda h, b: (h, side, b, 0, 0))
    flat = pl.BlockSpec((total_rows, width), lambda h, b: (0, 0))
    floor = pl.BlockSpec((None, block, rows, width), lambda h, b: (h, b, 0, 0))
    heat = pl.BlockSpec((rows, width), lambda h, b: (0, 0))
    in_specs = [whole(pltpu.SMEM)] * len(scalars) + [big, edge, edge, flat]
    flat_shape = jax.ShapeDtypeStruct((total_rows, width), F32)
    floor_shape = jax.ShapeDtypeStruct((half, modes, rows, width), F32)
    args = [*scalars, x, lo, hi, equil, start]
    if down:
        in_specs += [heat]
        out_shape = (jax.ShapeDtypeStruct(x.shape, F32), floor_shape, flat_shape)
        out_specs = (big, floor, flat)
        aliases = {}
    else:
        in_specs += [floor, flat, whole(pl.ANY)]
        args += [before, aliased]
        out_shape = (jax.ShapeDtypeStruct(x.shape, F32), flat_shape)
        out_specs = (big, flat)
        aliases = {len(args) - 1: 0}
    return pl.pallas_call(
        functools.partial(sweep_kernel, down, planes),
        grid=(half, modes // block),
        out_shape=out_shape,
        in_specs=in_specs,
        out_specs=out_specs,
        input_output_aliases=aliases,
        name="down_sweep" if down else "up_sweep",
    )(*args)


def per_device(
    n, ns, intensity, dir_cos, velocity, rate, spectrum, weight, heat, rough_cells, rough_count,
    rough_map,
):
    pairs, planes, rows, width = intensity.shape
    modes = velocity.shape[0]
    half = pairs // modes // 2
    pairs_total = pairs * n
    position = lax.axis_index("mode")
    flat = intensity.reshape(pairs, planes * rows, width)
    equil, lo, hi = open_step(flat, weight, n, ns, modes, planes, pairs_total)
    x = intensity.reshape(half, 2, modes, planes * rows, width)
    lo = lo.reshape(half, 2, modes, planes, width)
    hi = hi.reshape(half, 2, modes, planes, width)
    scalars = (dir_cos, velocity, rate, spectrum, weight)
    fresh, bottom, energy = sweep_step(True, planes, scalars, x, lo, hi, equil, heat)
    targets = lax.dynamic_slice_in_dim(rough_map, position * half, half, 1).T
    inflow = rough_step(
        bottom.reshape(half * modes, rows, width), rough_cells[None], rough_count, targets, n
    )
    inflow = inflow.reshape(half, modes, rows, width)
    fresh, energy = sweep_step(
        False, planes, scalars, x, lo, hi, equil, inflow, energy, fresh
    )
    energy = close_step(energy, n, pairs_total)
    return fresh.reshape(intensity.shape), energy.reshape(planes, rows, width)


def solution(mesh):
    n, ns = mesh.shape["mode"], mesh.shape["space"]
    in_specs = (
        P("mode", None, "space", None),
        P(),
        P(),
        P(),
        P(),
        P(),
        P("space", None),
        P("space"),
        P("space"),
        P("space", None),
    )
    out_specs = (P("mode", None, "space", None), P(None, "space", None))
    return jax.shard_map(
        functools.partial(per_device, n, ns),
        mesh=mesh,
        in_specs=in_specs,
        out_specs=out_specs,
        check_vma=False,
    )
```

```python
import functools

import jax
import jax.numpy as jnp
from jax import lax
from jax.experimental import pallas as pl
from jax.experimental.pallas import tpu as pltpu
from jax.sharding import PartitionSpec as P

MESH = pl.DeviceIdType.MESH
F32 = jnp.float32
BF16 = jnp.bfloat16


def whole(space=pltpu.VMEM):
    return pl.BlockSpec(memory_space=space)


def squash(energy):
    return energy / (1.0 + 0.3 * jnp.abs(energy))


def send(src, dst, ssem, rsem, axis, target):
    return pltpu.make_async_remote_copy(
        src_ref=src,
        dst_ref=dst,
        send_sem=ssem,
        recv_sem=rsem,
        device_id={axis: target},
        device_id_type=MESH,
    )


def reduce_all(acc, slots, part, total, sems, n, finish):
    me = lax.axis_index("mode")
    rows = acc.shape[0] // n

    def chunk(i):
        return pl.ds(pl.multiple_of(i * rows, rows), rows)

    first = []
    for off in range(1, n):
        target = lax.rem(me + off, n)
        copy = send(
            acc.at[chunk(target)], slots.at[off], sems.at[0, off], sems.at[1, off], "mode", target
        )
        copy.start()
        first.append(copy)
    for copy in first:
        copy.wait_recv()
    value = acc[chunk(me), :]
    for off in range(1, n):
        value = value + slots[off]
    part[...] = finish(value)
    second = []
    for off in range(1, n):
        target = lax.rem(me + off, n)
        copy = send(part, total.at[chunk(me)], sems.at[2, off], sems.at[3, off], "mode", target)
        copy.start()
        second.append(copy)
    total[chunk(me), :] = part[...]
    for copy in first:
        copy.wait_send()
    for off in range(1, n):
        source = lax.rem(me + n - off, n)
        send(
            part, total.at[chunk(source)], sems.at[2, off], sems.at[3, off], "mode", source
        ).wait_recv()
    for copy in second:
        copy.wait_send()


def greet_modes(barrier, n):
    me = lax.axis_index("mode")
    for off in range(1, n):
        pl.semaphore_signal(
            barrier, inc=1, device_id={"mode": lax.rem(me + off, n)}, device_id_type=MESH
        )


def open_kernel(
    n, ns, modes, planes, pairs_total,
    weight, x_ref, equil, lo_out, hi_out,
    acc, slots, part, total, row_first, row_last, hsem, sems,
):
    step = pl.program_id(0)
    steps = pl.num_programs(0)
    block = x_ref.shape[0]
    rows = x_ref.shape[1]
    per_plane = rows // planes
    me = lax.axis_index("mode")
    sp = lax.axis_index("space")
    dirs_local = lo_out.shape[0] // modes

    @pl.when(step == 0)
    def _():
        barrier = pltpu.get_barrier_semaphore()
        greet_modes(barrier, n)

        @pl.when(sp > 0)
        def _():
            pl.semaphore_signal(barrier, inc=1, device_id={"space": sp - 1}, device_id_type=MESH)

        @pl.when(sp < ns - 1)
        def _():
            pl.semaphore_signal(barrier, inc=1, device_id={"space": sp + 1}, device_id_type=MESH)

        low = jnp.where(sp > 0, 1, 0)
        high = jnp.where(sp < ns - 1, 1, 0)
        pl.semaphore_wait(barrier, n - 1 + low + high)
        acc[...] = jnp.zeros_like(acc)

    part_of = pl.ds(step * block, block)
    has_low = jnp.where(sp > 0, 1.0, 0.0)
    has_high = jnp.where(sp < ns - 1, 1.0, 0.0)

    def edges(p, carry):
        for z in range(planes):
            first, last = z * per_plane, (z + 1) * per_plane - 1
            row_first[step * block + p, pl.ds(z, 1), :] = x_ref[p, pl.ds(first, 1), :] * has_low
            row_last[step * block + p, pl.ds(z, 1), :] = x_ref[p, pl.ds(last, 1), :] * has_high
        return carry

    lax.fori_loop(0, block, edges, 0)

    def down_copy(g):
        where = pl.ds(g * block, block)
        return send(
            row_first.at[where], hi_out.at[where], hsem.at[0, g], hsem.at[1, g], "space",
            lax.rem(sp + ns - 1, ns),
        )

    def up_copy(g):
        where = pl.ds(g * block, block)
        return send(
            row_last.at[where], lo_out.at[where], hsem.at[2, g], hsem.at[3, g], "space",
            lax.rem(sp + 1, ns),
        )

    def low_zero(g):
        where = pl.ds(g * block, block)
        return pltpu.make_async_copy(row_first.at[where], lo_out.at[where], hsem.at[3, g])

    def high_zero(g):
        where = pl.ds(g * block, block)
        return pltpu.make_async_copy(row_last.at[where], hi_out.at[where], hsem.at[1, g])

    @pl.when(sp > 0)
    def _():
        down_copy(step).start()

    @pl.when(sp == 0)
    def _():
        low_zero(step).start()

    @pl.when(sp < ns - 1)
    def _():
        up_copy(step).start()

    @pl.when(sp == ns - 1)
    def _():
        high_zero(step).start()

    w = weight[me * dirs_local + step * block // modes]

    def add_rows(r, carry):
        here = pl.ds(pl.multiple_of(r * 8, 8), 8)
        value = x_ref[0, here, :]
        for p in range(1, block):
            value = value + x_ref[p, here, :]
        acc[here, :] += w * value
        return carry

    lax.fori_loop(0, rows // 8, add_rows, 0)

    @pl.when(step == steps - 1)
    def _():
        reduce_all(
            acc, slots, part, total, sems, n, lambda value: squash(value * (1.0 / pairs_total))
        )
        equil[...] = total[...]

        def finish(g, carry):
            @pl.when(sp > 0)
            def _():
                down_copy(g).wait_send()
                up_copy(g).wait_recv()

            @pl.when(sp == 0)
            def _():
                low_zero(g).wait()

            @pl.when(sp < ns - 1)
            def _():
                up_copy(g).wait_send()
                down_copy(g).wait_recv()

            @pl.when(sp == ns - 1)
            def _():
                high_zero(g).wait()

            return carry

        lax.fori_loop(0, lo_out.shape[0] // block, finish, 0)


def open_step(x, weight, n, ns, modes, planes, pairs_total):
    pairs, rows, width = x.shape
    block = 16
    halo = jax.ShapeDtypeStruct((pairs, planes, width), F32)
    return pl.pallas_call(
        functools.partial(open_kernel, n, ns, modes, planes, pairs_total),
        grid=(pairs // block,),
        out_shape=(jax.ShapeDtypeStruct((rows, width), F32), halo, halo),
        in_specs=[whole(pltpu.SMEM), pl.BlockSpec((block, rows, width), lambda i: (i, 0, 0))],
        out_specs=(pl.BlockSpec((rows, width), lambda i: (0, 0)), whole(pl.ANY), whole(pl.ANY)),
        scratch_shapes=[
            pltpu.VMEM((rows, width), F32),
            pltpu.VMEM((n, rows // n, width), F32),
            pltpu.VMEM((rows // n, width), F32),
            pltpu.VMEM((rows, width), F32),
            pltpu.VMEM((pairs, planes, width), F32),
            pltpu.VMEM((pairs, planes, width), F32),
            pltpu.SemaphoreType.DMA((4, pairs // block)),
            pltpu.SemaphoreType.DMA((4, n)),
        ],
        compiler_params=pltpu.CompilerParams(collective_id=0, has_side_effects=True),
        name="open_step",
    )(weight, x)


def close_kernel(n, pairs_total, x_ref, out, slots, part, total, sems):
    barrier = pltpu.get_barrier_semaphore()
    greet_modes(barrier, n)
    pl.semaphore_wait(barrier, n - 1)
    reduce_all(x_ref, slots, part, total, sems, n, lambda value: value * (1.0 / pairs_total))
    out[...] = total[...]


def close_step(x, n, pairs_total):
    rows, width = x.shape
    return pl.pallas_call(
        functools.partial(close_kernel, n, pairs_total),
        out_shape=jax.ShapeDtypeStruct((rows, width), F32),
        in_specs=[whole()],
        out_specs=whole(),
        scratch_shapes=[
            pltpu.VMEM((n, rows // n, width), F32),
            pltpu.VMEM((rows // n, width), F32),
            pltpu.VMEM((rows, width), F32),
            pltpu.SemaphoreType.DMA((4, n)),
        ],
        compiler_params=pltpu.CompilerParams(collective_id=1, has_side_effects=True),
        name="close_step",
    )(x)


def split(value):
    high = value.astype(BF16)
    return high, (value - high.astype(F32)).astype(BF16)


def rough_kernel(
    n, planes, count, dir_cos, velocity, rate, spectrum, bottom, cells, targets, equil, x, lo, hi,
    inflow, base, held, picked, marks, xin, loin, hiin, xout, ssem, rsem, lsem,
):
    me = lax.axis_index("mode")
    pairs, rows, width = bottom.shape
    slots = cells.shape[1]
    half = targets.shape[0]
    modes = pairs // half

    def place_of(index):
        return jnp.where(lax.rem(index, 2) == 0, index // 2, n - 1 - index // 2)

    def index_of(place):
        place = lax.rem(place + n, n)
        return jnp.where(place < n // 2, 2 * place, 2 * (n - 1 - place) + 1)

    place = place_of(me)
    ends = (index_of(place + 1), index_of(place - 1))
    barrier = pltpu.get_barrier_semaphore()
    for target in ends:
        pl.semaphore_signal(barrier, inc=1, device_id={"mode": target}, device_id_type=MESH)

    marks[...] = jnp.where(
        lax.broadcasted_iota(jnp.int32, (width, slots), 0) == lax.rem(cells[...], width), 1.0, 0.0
    ).astype(BF16)
    row_of = cells[...] // width
    on_row = jnp.where(lax.broadcasted_iota(jnp.int32, (rows, slots), 0) == row_of, 1.0, 0.0)

    piece = pairs // 4

    def rows_of(way, part):
        return (2 * way + part) * piece

    def gather(first):
        here = pl.ds(first, piece)
        high, low = split(bottom[here].reshape(piece * rows, width))
        column = marks[...]
        got = jnp.dot(high, column, preferred_element_type=F32) + jnp.dot(
            low, column, preferred_element_type=F32
        )
        held[place, here, :] = jnp.sum(got.reshape(piece, rows, slots) * on_row[None], axis=1)

    def slot_of(way, step):
        return lax.rem(place + n + (-step if way == 0 else step), n)

    def copy_of(way, part, step):
        at = held.at[slot_of(way, step), pl.ds(rows_of(way, part), piece)]
        return send(at, at, ssem.at[way, part, step], rsem.at[way, part, step], "mode", ends[way])

    def arrival(way, part, step):
        at = held.at[slot_of(way, step + 1), pl.ds(rows_of(way, part), piece)]
        return send(at, at, ssem.at[way, part, step], rsem.at[way, part, step], "mode", ends[way])

    def choose(way, step):
        slot = slot_of(way, step)
        owner = index_of(slot)
        for h in range(half):
            want = targets[pl.ds(h, 1), :]
            for first in range(rows_of(way, 0), rows_of(way, 0) + 2 * piece, 8):
                j, m = first // modes, first % modes
                here = pl.ds(h * modes + m, 8)
                picked[here, :] = jnp.where(
                    want == owner * half + j, held[slot, pl.ds(first, 8), :], picked[here, :]
                )

    batch = xin.shape[1]
    per_dir = modes // batch
    chunks = half * per_dir
    wide = min(4, batch)
    row = lax.broadcasted_iota(jnp.int32, (rows, width), 0)
    lane = lax.broadcasted_iota(jnp.int32, (rows, width), 1)

    def loads(c):
        at = (c // per_dir, 0, pl.ds((c % per_dir) * batch, batch))
        return [
            pltpu.make_async_copy(src.at[at], dst.at[c % 2], lsem.at[k, c % 2])
            for k, (src, dst) in enumerate(((x, xin), (lo, loin), (hi, hiin)))
        ]

    def store(c):
        at = (c // per_dir, pl.ds((c % per_dir) * batch, batch))
        return pltpu.make_async_copy(xout.at[c % 2], base.at[at], lsem.at[3, c % 2])

    def advance(c):
        for copy in loads(c):
            copy.wait()
        if c + 1 < chunks:
            for copy in loads(c + 1):
                copy.start()
        if c >= 2:
            store(c - 2).wait()
        slot = c % 2
        s = (me * half + c // per_dir) * 2
        cx, cy, cz = dir_cos[0, s], dir_cos[1, s], dir_cos[2, s]
        low_x = jnp.full((rows, width), cx, F32) >= 0.0
        low_y = jnp.full((rows, width), cy, F32) >= 0.0
        at_edge = (low_x & (row == 0)) | (~low_x & (row == rows - 1))
        at_side = (low_y & (lane == 0)) | (~low_y & (lane == width - 1))

        def some(g, carry):
            picks = [g * wide + t for t in range(wide)]
            own_k, x_k, y_k, src_k, prev_k, values = [], [], [], [], [], [None] * wide
            for i in picks:
                m = (c % per_dir) * batch + i
                v = velocity[m]
                turn = v * jnp.abs(cz)
                inv = 1.0 / jnp.full((rows, width), 1.0 + rate[m] + turn, F32)
                vx, vy = v * jnp.abs(cx), v * jnp.abs(cy)
                own_k.append(inv * (1.0 - vx - vy))
                x_k.append(inv * vx)
                y_k.append(inv * vy)
                src_k.append(inv * (rate[m] * spectrum[m]))
                prev_k.append(inv * turn)
            for z in range(planes):
                here = pl.ds(z * rows, rows)
                level = equil[here, :]
                for t, i in enumerate(picks):
                    own = xin[slot, i, here, :]
                    edge = jnp.where(
                        low_x,
                        jnp.broadcast_to(loin[slot, i, pl.ds(z, 1), :], (rows, width)),
                        jnp.broadcast_to(hiin[slot, i, pl.ds(z, 1), :], (rows, width)),
                    )
                    side = jnp.where(low_x, pltpu.roll(own, 1, 0), pltpu.roll(own, rows - 1, 0))
                    side = jnp.where(at_edge, edge, side)
                    along = jnp.where(low_y, pltpu.roll(own, 1, 1), pltpu.roll(own, width - 1, 1))
                    along = jnp.where(at_side, 0.0, along)
                    value = (
                        own_k[t] * own + x_k[t] * side + y_k[t] * along + src_k[t] * level
                    )
                    if values[t] is not None:
                        value = value + prev_k[t] * values[t]
                    values[t] = value
                    xout[slot, i, here, :] = value
            return carry

        lax.fori_loop(0, batch // wide, some, 0)
        store(c).start()

    for copy in loads(0):
        copy.start()
    for part in range(2):
        for way in range(2):
            gather(rows_of(way, part))
            if part == 0 and way == 0:
                pl.semaphore_wait(barrier, 2)
            copy_of(way, part, 0).start()
    picked[...] = jnp.zeros_like(picked)
    for way in range(2):
        choose(way, 0)
    for c in range(0, chunks // n):
        advance(c)
    for step in range(1, n):
        for part in range(2):
            for way in range(2):
                arrival(way, part, step - 1).wait_recv()
                if step < n - 1:
                    copy_of(way, part, step).start()
        for way in range(2):
            choose(way, step)
        for c in range(step * chunks // n, (step + 1) * chunks // n):
            advance(c)
    for step in range(n - 1):
        for part in range(2):
            for way in range(2):
                copy_of(way, part, step).wait_send()

    for c in range(max(0, chunks - 2), chunks):
        store(c).wait()
    group = piece
    live = jnp.where(lax.broadcasted_iota(jnp.int32, (rows, slots), 1) < count[0], on_row, 0.0)
    contract = (((1,), (1,)), ((), ()))
    is_rough = lax.dot_general(live.astype(BF16), marks[...], contract, preferred_element_type=F32)
    is_rough = (is_rough > 0.5)[None]

    def scatter(g, carry):
        here = pl.ds(pl.multiple_of(g * group, group), group)
        spread = (picked[here, :][:, None, :] * live[None]).reshape(group * rows, slots)
        high, low = split(spread)
        column = marks[...]
        put = lax.dot_general(
            high, column, contract, preferred_element_type=F32
        ) + lax.dot_general(low, column, contract, preferred_element_type=F32)
        inflow[here] = 0.9 * jnp.where(is_rough, put.reshape(group, rows, width), bottom[here])
        return carry

    lax.fori_loop(0, pairs // group, scatter, 0)


def rough_step(bottom, cells, count, targets, scalars, equil, x, lo, hi, n):
    pairs, rows, width = bottom.shape
    slots = cells.shape[1]
    half, _, modes, total_rows, _ = x.shape
    planes = total_rows // rows
    batch = min(8, modes)
    return pl.pallas_call(
        functools.partial(rough_kernel, n, planes),
        out_shape=(
            jax.ShapeDtypeStruct(bottom.shape, F32),
            jax.ShapeDtypeStruct((half, modes, total_rows, width), F32),
        ),
        in_specs=[whole(pltpu.SMEM)] * 5 + [whole()] * 4 + [whole(pl.ANY)] * 3,
        out_specs=(whole(), whole(pl.ANY)),
        scratch_shapes=[
            pltpu.VMEM((n, pairs, slots), F32),
            pltpu.VMEM((pairs, slots), F32),
            pltpu.VMEM((width, slots), BF16),
            pltpu.VMEM((2, batch, total_rows, width), F32),
            pltpu.VMEM((2, batch, planes, width), F32),
            pltpu.VMEM((2, batch, planes, width), F32),
            pltpu.VMEM((2, batch, total_rows, width), F32),
            pltpu.SemaphoreType.DMA((2, 2, n - 1)),
            pltpu.SemaphoreType.DMA((2, 2, n - 1)),
            pltpu.SemaphoreType.DMA((4, 2)),
        ],
        compiler_params=pltpu.CompilerParams(collective_id=2, has_side_effects=True),
        name="rough_step",
    )(count, *scalars[:4], bottom, cells, targets, equil, x, lo, hi)


def rise_kernel(planes, dir_cos, velocity, rate, weight, base, inflow, before, _, out, energy):
    h, b = pl.program_id(0), pl.program_id(1)
    count, total_rows, width = base.shape
    rows = total_rows // planes

    @pl.when((h == 0) & (b == 0))
    def _():
        energy[...] = before[...]

    s = (lax.axis_index("mode") * pl.num_programs(0) + h) * 2
    cz, w = dir_cos[2, s], weight[s]
    wide = min(4, count)

    def some(g, carry):
        picks = [g * wide + t for t in range(wide)]
        prev_k, values = [], []
        for i in picks:
            m = b * count + i
            turn = velocity[m] * jnp.abs(cz)
            ratio = jnp.full((rows, width), turn, F32) / jnp.full(
                (rows, width), 1.0 + rate[m] + turn, F32
            )
            prev_k.append(ratio)
            values.append(inflow[i])
        for z in range(planes):
            here = pl.ds(z * rows, rows)
            total = None
            for t, i in enumerate(picks):
                values[t] = prev_k[t] * values[t]
                value = base[i, here, :] + values[t]
                out[i, here, :] = value
                total = value if total is None else total + value
            energy[here, :] += w * total
        return carry

    lax.fori_loop(0, count // wide, some, 0)


def rise_step(planes, scalars, base, inflow, before, fresh):
    half, modes, total_rows, width = base.shape
    rows = total_rows // planes
    block = min(8, modes)
    dir_cos, velocity, rate, _, weight = scalars
    flat = pl.BlockSpec((total_rows, width), lambda h, b: (0, 0))
    return pl.pallas_call(
        functools.partial(rise_kernel, planes),
        grid=(half, modes // block),
        out_shape=(
            jax.ShapeDtypeStruct(fresh.shape, F32),
            jax.ShapeDtypeStruct((total_rows, width), F32),
        ),
        in_specs=[whole(pltpu.SMEM)] * 4
        + [
            pl.BlockSpec((None, block, total_rows, width), lambda h, b: (h, b, 0, 0)),
            pl.BlockSpec((None, block, rows, width), lambda h, b: (h, b, 0, 0)),
            flat,
            whole(pl.ANY),
        ],
        out_specs=(
            pl.BlockSpec((None, None, block, total_rows, width), lambda h, b: (h, 0, b, 0, 0)),
            flat,
        ),
        input_output_aliases={7: 0},
        name="rise_step",
    )(dir_cos, velocity, rate, weight, base, inflow, before, fresh)


def sweep_kernel(down, planes, *refs):
    if down:
        (dir_cos, velocity, rate, spectrum, weight, x_ref, lo, hi, equil, start, out, bottom,
         energy) = refs
    else:
        (dir_cos, velocity, rate, spectrum, weight, x_ref, lo, hi, equil, start, before, _,
         out, energy) = refs
    h, b = pl.program_id(0), pl.program_id(1)
    count, total_rows, width = x_ref.shape
    rows = total_rows // planes

    @pl.when((h == 0) & (b == 0))
    def _():
        energy[...] = jnp.zeros_like(energy) if down else before[...]

    s = (lax.axis_index("mode") * pl.num_programs(0) + h) * 2 + (1 if down else 0)
    cx, cy, cz = dir_cos[0, s], dir_cos[1, s], dir_cos[2, s]
    w = weight[s]
    row = lax.broadcasted_iota(jnp.int32, (rows, width), 0)
    lane = lax.broadcasted_iota(jnp.int32, (rows, width), 1)

    wide = min(4, count)

    def run(low_x, low_y):
        def some(g, carry):
            picks = [g * wide + t for t in range(wide)]
            own_k, x_k, y_k, src_k, prev_k, values = [], [], [], [], [], []
            for i in picks:
                m = b * count + i
                v = velocity[m]
                c = v * jnp.abs(cz)
                inv = 1.0 / jnp.full((rows, width), 1.0 + rate[m] + c, F32)
                vx, vy = v * jnp.abs(cx), v * jnp.abs(cy)
                own_k.append(inv * (1.0 - vx - vy))
                x_k.append(inv * vx)
                y_k.append(inv * vy)
                src_k.append(inv * (rate[m] * spectrum[m]))
                prev_k.append(inv * c)
                values.append(start[...] * spectrum[m] if down else start[i])
            for z in reversed(range(planes)) if down else range(planes):
                here = pl.ds(z * rows, rows)
                level = equil[here, :]
                total = None
                for t, i in enumerate(picks):
                    own = x_ref[i, here, :]
                    edge = (lo if low_x else hi)[i, pl.ds(z, 1), :]
                    if low_x:
                        side = jnp.where(row == 0, edge, pltpu.roll(own, 1, 0))
                    else:
                        side = jnp.where(row == rows - 1, edge, pltpu.roll(own, rows - 1, 0))
                    along = pltpu.roll(own, 1 if low_y else width - 1, 1)
                    along = jnp.where(lane == (0 if low_y else width - 1), 0.0, along)
                    value = (
                        own_k[t] * own + x_k[t] * side + y_k[t] * along + src_k[t] * level
                        + prev_k[t] * values[t]
                    )
                    values[t] = value
                    out[i, here, :] = value
                    total = value if total is None else total + value
                energy[here, :] += w * total
            if down:
                for t, i in enumerate(picks):
                    bottom[i] = values[t]
            return carry

        lax.fori_loop(0, count // wide, some, 0)

    for low_x in (True, False):
        for low_y in (True, False):
            @pl.when(((cx >= 0) == low_x) & ((cy >= 0) == low_y))
            def _():
                run(low_x, low_y)


def sweep_step(down, planes, scalars, x, lo, hi, equil, start, before=None, aliased=None):
    half, _, modes, total_rows, width = x.shape
    rows = total_rows // planes
    block = min(8, modes)
    side = 1 if down else 0
    big = pl.BlockSpec((None, None, block, total_rows, width), lambda h, b: (h, side, b, 0, 0))
    edge = pl.BlockSpec((None, None, block, planes, width), lambda h, b: (h, side, b, 0, 0))
    flat = pl.BlockSpec((total_rows, width), lambda h, b: (0, 0))
    floor = pl.BlockSpec((None, block, rows, width), lambda h, b: (h, b, 0, 0))
    heat = pl.BlockSpec((rows, width), lambda h, b: (0, 0))
    in_specs = [whole(pltpu.SMEM)] * len(scalars) + [big, edge, edge, flat]
    flat_shape = jax.ShapeDtypeStruct((total_rows, width), F32)
    floor_shape = jax.ShapeDtypeStruct((half, modes, rows, width), F32)
    args = [*scalars, x, lo, hi, equil, start]
    if down:
        in_specs += [heat]
        out_shape = (jax.ShapeDtypeStruct(x.shape, F32), floor_shape, flat_shape)
        out_specs = (big, floor, flat)
        aliases = {}
    else:
        in_specs += [floor, flat, whole(pl.ANY)]
        args += [before, aliased]
        out_shape = (jax.ShapeDtypeStruct(x.shape, F32), flat_shape)
        out_specs = (big, flat)
        aliases = {len(args) - 1: 0}
    return pl.pallas_call(
        functools.partial(sweep_kernel, down, planes),
        grid=(half, modes // block),
        out_shape=out_shape,
        in_specs=in_specs,
        out_specs=out_specs,
        input_output_aliases=aliases,
        name="down_sweep" if down else "up_sweep",
    )(*args)


def per_device(
    n, ns, intensity, dir_cos, velocity, rate, spectrum, weight, heat, rough_cells, rough_count,
    rough_map,
):
    pairs, planes, rows, width = intensity.shape
    modes = velocity.shape[0]
    half = pairs // modes // 2
    pairs_total = pairs * n
    position = lax.axis_index("mode")
    flat = intensity.reshape(pairs, planes * rows, width)
    equil, lo, hi = open_step(flat, weight, n, ns, modes, planes, pairs_total)
    x = intensity.reshape(half, 2, modes, planes * rows, width)
    lo = lo.reshape(half, 2, modes, planes, width)
    hi = hi.reshape(half, 2, modes, planes, width)
    scalars = (dir_cos, velocity, rate, spectrum, weight)
    fresh, bottom, energy = sweep_step(True, planes, scalars, x, lo, hi, equil, heat)
    targets = lax.dynamic_slice_in_dim(rough_map, position * half, half, 1).T
    inflow, base = rough_step(
        bottom.reshape(half * modes, rows, width), rough_cells[None], rough_count, targets,
        scalars, equil, x, lo, hi, n,
    )
    inflow = inflow.reshape(half, modes, rows, width)
    fresh, energy = rise_step(planes, scalars, base, inflow, energy, fresh)
    energy = close_step(energy, n, pairs_total)
    return fresh.reshape(intensity.shape), energy.reshape(planes, rows, width)


def solution(mesh):
    n, ns = mesh.shape["mode"], mesh.shape["space"]
    in_specs = (
        P("mode", None, "space", None),
        P(),
        P(),
        P(),
        P(),
        P(),
        P("space", None),
        P("space"),
        P("space"),
        P("space", None),
    )
    out_specs = (P("mode", None, "space", None), P(None, "space", None))
    return jax.shard_map(
        functools.partial(per_device, n, ns),
        mesh=mesh,
        in_specs=in_specs,
        out_specs=out_specs,
        check_vma=False,
    )
```
